32 devices in a mesh: fsdp: 8 (over z, y), ctx: 4 (over x, core).
Axes of the slice: x: 2, y: 2, z: 4, core: 2. Of those that a mesh axis runs over, the one named last changes fastest.
Arguments:
- tokens: bfloat16 [2, 8, 512, 512], P(None, 'fsdp', 'ctx'), may hold values from -6 to 6
- lengths: int32 [2, 8], P(None, 'fsdp'), may hold values from 8 to 512, as said below
- cotangent: bfloat16 [2, 8, 512, 512], P(None, 'fsdp', 'ctx'), may hold values from -6 to 6
- first_up: bfloat16 [512, 2048], P('fsdp'), may hold values from -0.25 to 0.25
- first_down: bfloat16 [2048, 512], P('fsdp'), may hold values from -0.125 to 0.125
- project_in: bfloat16 [512, 1536], P('fsdp'), may hold values from -0.25 to 0.25
- project_out: bfloat16 [512, 512], P('fsdp'), may hold values from -1 to 1
- pointwise_in: bfloat16 [512, 1024], P('fsdp'), may hold values from -0.25 to 0.25
- depthwise: bfloat16 [512, 31], P('fsdp'), may hold values from -1 to 1
- pointwise_out: bfloat16 [512, 512], P('fsdp'), may hold values from -0.25 to 0.25
- second_up: bfloat16 [512, 2048], P('fsdp'), may hold values from -0.25 to 0.25
- second_down: bfloat16 [2048, 512], P('fsdp'), may hold values from -0.125 to 0.125
- gains: bfloat16 [6, 512], P(None, 'fsdp'), may hold values from 0.25 to 1.75
- batch_shift: bfloat16 [512], P('fsdp'), may hold values from -3 to 3
- head_terms: float32 [2, 8], replicated, may hold values from -3 to 300, as said below
Outputs:
- output: bfloat16 [2, 8, 512, 512], P(None, 'fsdp', 'ctx')
- grad_tokens: bfloat16 [2, 8, 512, 512], P(None, 'fsdp', 'ctx')
- grad_first_up: float32 [512, 2048], P('fsdp')
- grad_first_down: float32 [2048, 512], P('fsdp')
- grad_project_in: float32 [512, 1536], P('fsdp')
- grad_project_out: float32 [512, 512], P('fsdp')
- grad_pointwise_in: float32 [512, 1024], P('fsdp')
- grad_depthwise: float32 [512, 31], P('fsdp')
- grad_pointwise_out: float32 [512, 512], P('fsdp')
- grad_second_up: float32 [512, 2048], P('fsdp')
- grad_second_down: float32 [2048, 512], P('fsdp')
- grad_gains: float32 [6, 512], P(None, 'fsdp')
- grad_batch_shift: float32 [512], P('fsdp')
- grad_head_terms: float32 [2, 8], replicated
The draws below stay inside these ranges and needn't reach their ends.
Inputs may be any that keep to these rules, and one draw needn't show every extreme that they name: `lengths`: the first sequence of every micro-batch has all 512 frames. `head_terms`: row 0 is positive.
All inputs are finite; a program needn't handle non-finite values.
Results may differ from the reference program's by a relative error of at most 0.02.
Values may be sent and summed in bfloat16 or wider, within the bound.
A program may use at most 128 MiB of HBM per device.

```python
import math
import jax
import jax.numpy as jnp
from jax import lax

D = 512
H = 8
FF = 2048
KW = 31
HD = 64
LMAX = 512
RFAR = 256
MB = 2
NSEQ = 8


def draw_lengths(key, part):
    values = jax.random.randint(key, (MB, NSEQ), 8, LMAX + 1)
    return values.at[:, 0].set(LMAX).astype(jnp.int32)


def draw_head_terms(key, part):
    slope_key, far_key = jax.random.split(jax.random.fold_in(key, 17))
    slopes = jnp.exp(jax.random.uniform(slope_key, (H,), jnp.float32, math.log(0.002), math.log(0.15)))
    far = jax.random.uniform(far_key, (H,), jnp.float32, -3.0, 3.0)
    return jnp.stack([slopes, far]).astype(jnp.float32)


def level_of(key, shape, cuts, low, top_value):
    factor_of, own = 1.0, jax.random.fold_in(key, 6)
    for dim, blocks in cuts:
        heights = jnp.exp(jax.random.uniform(jax.random.fold_in(own, dim), (blocks,), jnp.float32, low / len(cuts), top_value / len(cuts)))
        factor_of = factor_of * jnp.repeat(heights, shape[dim] // blocks).reshape([-1 if axis == dim else 1 for axis in range(len(shape))])
    return factor_of


def bell_draw(own_key, dims, scale, limit, pieces=(), kind=jnp.bfloat16):
    loudness = level_of(own_key, dims, pieces, -0.22, 0.18) if pieces else 1.0
    array = jax.random.normal(own_key, dims, jnp.float32) * scale * loudness
    return jnp.minimum(jnp.maximum(array, -limit), limit).astype(kind)


def setup_inputs(seed: int = 0) -> dict:
    streams_of = jax.random.split(jax.random.key(seed), 16)
    return {
        "tokens": bell_draw(streams_of[0], (MB, NSEQ, LMAX, D), 1.0, 6.0, ((1, 8), (2, 4))),
        "lengths": draw_lengths(jax.random.fold_in(streams_of[15], 71), 0),
        "cotangent": bell_draw(streams_of[2], (MB, NSEQ, LMAX, D), 1.0, 6.0, ((1, 8), (2, 4))),
        "first_up": bell_draw(streams_of[3], (D, FF), D ** -0.5, 0.25, ((0, 8),)),
        "first_down": bell_draw(streams_of[4], (FF, D), FF ** -0.5, 0.125, ((0, 8),)),
        "project_in": bell_draw(streams_of[5], (D, 3 * D), D ** -0.5, 0.25, ((0, 8),)),
        "project_out": bell_draw(streams_of[6], (D, D), (D // 16) ** -0.5, 1.0, ((0, 8),)),
        "pointwise_in": bell_draw(streams_of[7], (D, 2 * D), D ** -0.5, 0.25, ((0, 8),)),
        "depthwise": bell_draw(streams_of[8], (D, KW), KW ** -0.5, 1.0, ((0, 8),)),
        "pointwise_out": bell_draw(streams_of[9], (D, D), D ** -0.5, 0.25, ((0, 8),)),
        "second_up": bell_draw(streams_of[10], (D, FF), D ** -0.5, 0.25, ((0, 8),)),
        "second_down": bell_draw(streams_of[11], (FF, D), FF ** -0.5, 0.125, ((0, 8),)),
        "gains": jnp.clip(1.0 + 0.15 * jax.random.normal(streams_of[12], (6, D), jnp.float32), 0.25, 1.75).astype(jnp.bfloat16),
        "batch_shift": bell_draw(streams_of[13], (D,), 0.5, 3.0, ((0, 8),)),
        "head_terms": draw_head_terms(jax.random.fold_in(streams_of[15], 71), 0),
    }


EPS = 1e-05
NEGATIVE = -1e+30

def product(left, right):
    return jnp.dot(left, right, preferred_element_type=jnp.float32)

def product_left(left, right):
    return jnp.dot(left.T, right, preferred_element_type=jnp.float32)

def product_right(left, right):
    return jnp.dot(left, right.T, preferred_element_type=jnp.float32)

def swish(value):
    return value * jax.nn.sigmoid(value)

def swish_slope(value):
    sigma = jax.nn.sigmoid(value)
    return sigma * (1.0 + value * (1.0 - sigma))

def layer_norm(stream, gain):
    centred = stream - lax.optimization_barrier(jnp.mean(stream, axis=-1, keepdims=True))
    inverse = lax.rsqrt(lax.optimization_barrier(jnp.mean(centred * centred, axis=-1, keepdims=True)) + EPS)
    unit = centred * inverse
    return ((unit * gain).astype(jnp.bfloat16), unit, inverse)

def norm_back(dnormed, unit, inverse, gain):
    scaled = dnormed * gain
    dstream = inverse * (scaled - lax.optimization_barrier(jnp.mean(scaled, axis=-1, keepdims=True)) - unit * lax.optimization_barrier(jnp.mean(scaled * unit, axis=-1, keepdims=True)))
    return (dstream, lax.optimization_barrier(jnp.sum(dnormed * unit, axis=0)))

def position_terms(query_start, rows, keys, head_terms):
    query_pos = query_start + lax.iota(jnp.int32, rows)
    key_pos = lax.iota(jnp.int32, keys)
    offset = query_pos[:, None] - key_pos[None, :]
    distance = jnp.abs(offset).astype(jnp.float32)
    far = (offset >= RFAR).astype(jnp.float32)
    bias = far[None] * head_terms[1][:, None, None] - distance[None] * head_terms[0][:, None, None]
    return (bias, distance, far)

def split_heads(queries, keyvals):
    rows, width = queries.shape
    keys = keyvals.shape[0]
    query_heads = queries.reshape(rows, H, HD).astype(jnp.float32)
    key_heads = keyvals[:, :width].reshape(keys, H, HD).astype(jnp.float32)
    value_heads = keyvals[:, width:].reshape(keys, H, HD).astype(jnp.float32)
    return (query_heads, key_heads, value_heads)

def score_heads(query_heads, key_heads, bias, key_valid):
    scores = jnp.einsum('qhd,khd->hqk', query_heads, key_heads)
    scores = scores * HD ** (-0.5) + bias
    return jnp.where(key_valid[None, None, :], scores, NEGATIVE)

def attend_forward(queries, keyvals, bias, key_valid):
    rows, width = queries.shape
    query_heads, key_heads, value_heads = split_heads(queries, keyvals)
    scores = score_heads(query_heads, key_heads, bias, key_valid)
    top = lax.optimization_barrier(jnp.max(scores, axis=-1, keepdims=True))
    logsum = top + jnp.log(lax.optimization_barrier(jnp.sum(jnp.exp(scores - top), axis=-1, keepdims=True)))
    probs = jnp.exp(scores - logsum).astype(jnp.bfloat16)
    context = jnp.einsum('hqk,khd->qhd', probs.astype(jnp.float32), value_heads)
    return (context.reshape(rows, width).astype(jnp.bfloat16), logsum)

def attend_backward(queries, keyvals, bias, distance, far, key_valid, logsum, dcontext):
    rows, width = queries.shape
    keys = keyvals.shape[0]
    query_heads, key_heads, value_heads = split_heads(queries, keyvals)
    scores = score_heads(query_heads, key_heads, bias, key_valid)
    probs = jnp.exp(scores - logsum)
    dcontext_heads = dcontext.reshape(rows, H, HD).astype(jnp.float32)
    dprobs = jnp.einsum('qhd,khd->hqk', dcontext_heads, value_heads)
    dscores = probs * (dprobs - lax.optimization_barrier(jnp.sum(probs * dprobs, axis=-1, keepdims=True)))
    slope_grad = -lax.optimization_barrier(jnp.sum(dscores * distance[None], axis=(1, 2)))
    far_grad = lax.optimization_barrier(jnp.sum(dscores * far[None], axis=(1, 2)))
    dscores_low = dscores.astype(jnp.bfloat16).astype(jnp.float32)
    probs_low = probs.astype(jnp.bfloat16).astype(jnp.float32)
    factor = HD ** (-0.5)
    dquery = jnp.einsum('hqk,khd->qhd', dscores_low, key_heads) * factor
    dkey = jnp.einsum('hqk,qhd->khd', dscores_low, query_heads) * factor
    dvalue = jnp.einsum('hqk,qhd->khd', probs_low, dcontext_heads)
    dkeyvals = jnp.concatenate([dkey.reshape(keys, width), dvalue.reshape(keys, width)], axis=1)
    return (dquery.reshape(rows, width), dkeyvals, jnp.stack([slope_grad, far_grad]))

def depthwise_apply(padded, kernel, count):
    kernel_f = kernel.astype(jnp.float32)
    padded_f = padded.astype(jnp.float32)
    total = jnp.zeros(padded.shape[:-2] + (count, padded.shape[-1]), jnp.float32)
    for tap in range(kernel.shape[1]):
        total = total + padded_f[..., tap:tap + count, :] * kernel_f[:, tap]
    return total

def depthwise_back(padded, dpadded, ddepth, kernel, count):
    kernel_f = kernel.astype(jnp.float32)
    padded_f = padded.astype(jnp.float32)
    span = kernel.shape[1] - 1
    dgated = jnp.zeros(ddepth.shape, jnp.float32)
    columns = []
    for tap in range(kernel.shape[1]):
        dgated = dgated + dpadded[..., span - tap:span - tap + count, :] * kernel_f[:, tap]
        columns.append(lax.optimization_barrier(jnp.sum((padded_f[..., tap:tap + count, :] * ddepth).reshape(-1, kernel.shape[0]), axis=0)))
    return (dgated, jnp.stack(columns, axis=1))

def front_pass(x_seq, length, weights, bias, half):
    first_up, first_down, project_in, project_out, pointwise_in, depthwise, pointwise_out, second_up, second_down, gains, batch_shift = weights
    gain_rows = gains.astype(jnp.float32)
    frames, width = x_seq.shape
    valid = lax.iota(jnp.int32, frames) < length
    mask = valid.astype(jnp.float32)[:, None]
    stream_in = x_seq.astype(jnp.float32)
    normed_first, unit_first, inverse_first = layer_norm(stream_in, gain_rows[0])
    up_first = product(normed_first, first_up)
    act_first = swish(up_first).astype(jnp.bfloat16)
    stream_first = stream_in + 0.5 * product(act_first, first_down)
    normed_attend, unit_attend, inverse_attend = layer_norm(stream_first, gain_rows[1])
    triple = product(normed_attend, project_in).astype(jnp.bfloat16)
    context, logsum = attend_forward(triple[:, :width], triple[:, width:], bias, valid)
    stream_attend = stream_first + product(context, project_out)
    normed_conv, unit_conv, inverse_conv = layer_norm(stream_attend, gain_rows[2])
    expanded = product(normed_conv, pointwise_in)
    linear = expanded[:, :width]
    gate_sigma = jax.nn.sigmoid(expanded[:, width:])
    gated_low = (linear * gate_sigma * mask).astype(jnp.bfloat16)
    padded = jnp.pad(gated_low, ((half, half), (0, 0)))
    depth = depthwise_apply(padded, depthwise, frames)
    return {'valid': valid, 'mask': mask, 'stream_in': stream_in, 'normed_first': normed_first, 'unit_first': unit_first, 'inverse_first': inverse_first, 'up_first': up_first, 'act_first': act_first, 'normed_attend': normed_attend, 'unit_attend': unit_attend, 'inverse_attend': inverse_attend, 'triple': triple, 'context': context, 'logsum': logsum, 'stream_attend': stream_attend, 'normed_conv': normed_conv, 'unit_conv': unit_conv, 'inverse_conv': inverse_conv, 'linear': linear, 'gate_sigma': gate_sigma, 'padded': padded, 'depth': depth}

def reference(tokens, lengths, cotangent, first_up, first_down, project_in, project_out, pointwise_in, depthwise, pointwise_out, second_up, second_down, gains, batch_shift, head_terms):
    weights = (first_up, first_down, project_in, project_out, pointwise_in, depthwise, pointwise_out, second_up, second_down, gains, batch_shift)
    half = KW // 2
    frames = LMAX
    width = D
    bias, distance, far = position_terms(0, frames, frames, head_terms)
    positions = lax.iota(jnp.int32, frames)
    gain_rows = gains.astype(jnp.float32)
    shift_row = batch_shift.astype(jnp.float32)
    outputs = []
    dinputs = []
    totals = None
    for micro in range(MB):
        batch_tokens = tokens[micro]
        batch_lengths = lengths[micro]
        batch_cot = cotangent[micro]

        def first_scan(item):
            state = front_pass(item[0], item[1], weights, bias, half)
            return (state['depth'], state['stream_attend'])
        depths, streams = lax.map(first_scan, (batch_tokens, batch_lengths))
        masks = (positions[None, :] < batch_lengths[:, None]).astype(jnp.float32)[:, :, None]
        count = jnp.sum(masks)
        bn_mean = lax.optimization_barrier(jnp.sum(masks * depths, axis=(0, 1))) / count
        centred = depths - bn_mean
        inverse_bn = lax.rsqrt(lax.optimization_barrier(jnp.sum(masks * centred * centred, axis=(0, 1))) / count + EPS)
        units_bn = centred * inverse_bn

        def rear_step(carry, item):
            unit_bn, stream_attend, dout_low = item
            shifted = unit_bn * gain_rows[5] + shift_row
            act_conv = swish(shifted).astype(jnp.bfloat16)
            stream_conv = stream_attend + product(act_conv, pointwise_out)
            normed_second, unit_second, inverse_second = layer_norm(stream_conv, gain_rows[3])
            up_second = product(normed_second, second_up)
            act_second = swish(up_second).astype(jnp.bfloat16)
            stream_second = stream_conv + 0.5 * product(act_second, second_down)
            out_low, unit_out, inverse_out = layer_norm(stream_second, gain_rows[4])
            dsecond_stream, gain_out = norm_back(dout_low.astype(jnp.float32), unit_out, inverse_out, gain_rows[4])
            dsecond_low = (0.5 * dsecond_stream).astype(jnp.bfloat16)
            dup_second = (product_right(dsecond_low, second_down) * swish_slope(up_second)).astype(jnp.bfloat16)
            dtemp, gain_second = norm_back(product_right(dup_second, second_up), unit_second, inverse_second, gain_rows[3])
            dconv_stream = dsecond_stream + dtemp
            dconv_low = dconv_stream.astype(jnp.bfloat16)
            dshift = product_right(dconv_low, pointwise_out) * swish_slope(shifted)
            step = (product_left(normed_second, dup_second), product_left(act_second, dsecond_low), product_left(act_conv, dconv_low), gain_second, gain_out, lax.optimization_barrier(jnp.sum(dshift * unit_bn, axis=0)), lax.optimization_barrier(jnp.sum(dshift, axis=0)))
            return (tuple((old + new for old, new in zip(carry, step))), (out_low, dshift, dconv_stream))
        rear_init = (jnp.zeros((width, FF), jnp.float32), jnp.zeros((FF, width), jnp.float32), jnp.zeros((width, width), jnp.float32), jnp.zeros((width,), jnp.float32), jnp.zeros((width,), jnp.float32), jnp.zeros((width,), jnp.float32), jnp.zeros((width,), jnp.float32))
        rear_sums, (out_lows, dshifts, dconv_streams) = lax.scan(rear_step, rear_init, (units_bn, streams, batch_cot))
        sum_shift = lax.optimization_barrier(jnp.sum(dshifts, axis=(0, 1)))
        sum_cross = lax.optimization_barrier(jnp.sum(dshifts * units_bn, axis=(0, 1)))

        def lower_step(carry, item):
            x_seq, length, unit_bn, dshift, dconv_stream = item
            state = front_pass(x_seq, length, weights, bias, half)
            mask = state['mask']
            ddepth = inverse_bn * gain_rows[5] * (dshift - mask * sum_shift / count - mask * unit_bn * sum_cross / count)
            dpadded = jnp.pad(ddepth, ((half, half), (0, 0)))
            dgated, grad_depth = depthwise_back(state['padded'], dpadded, ddepth, depthwise, frames)
            dgated = dgated * mask
            gate_sigma = state['gate_sigma']
            dexpanded = jnp.concatenate([dgated * gate_sigma, dgated * state['linear'] * gate_sigma * (1.0 - gate_sigma)], axis=1).astype(jnp.bfloat16)
            dtemp, gain_conv = norm_back(product_right(dexpanded, pointwise_in), state['unit_conv'], state['inverse_conv'], gain_rows[2])
            dattend_stream = dconv_stream + dtemp
            dattend_low = dattend_stream.astype(jnp.bfloat16)
            dcontext = product_right(dattend_low, project_out).astype(jnp.bfloat16)
            triple = state['triple']
            dquery, dkeyvals, dheads = attend_backward(triple[:, :width], triple[:, width:], bias, distance, far, state['valid'], state['logsum'], dcontext)
            dtriple = jnp.concatenate([dquery, dkeyvals], axis=1).astype(jnp.bfloat16)
            dtemp, gain_attend = norm_back(product_right(dtriple, project_in), state['unit_attend'], state['inverse_attend'], gain_rows[1])
            dfirst_stream = dattend_stream + dtemp
            dfirst_low = (0.5 * dfirst_stream).astype(jnp.bfloat16)
            dup_first = (product_right(dfirst_low, first_down) * swish_slope(state['up_first'])).astype(jnp.bfloat16)
            dtemp, gain_first = norm_back(product_right(dup_first, first_up), state['unit_first'], state['inverse_first'], gain_rows[0])
            dinput = (dfirst_stream + dtemp).astype(jnp.bfloat16)
            step = (product_left(state['normed_first'], dup_first), product_left(state['act_first'], dfirst_low), product_left(state['normed_attend'], dtriple), product_left(state['context'], dattend_low), product_left(state['normed_conv'], dexpanded), grad_depth, gain_first, gain_attend, gain_conv, dheads)
            return (tuple((old + new for old, new in zip(carry, step))), dinput)
        lower_init = (jnp.zeros((width, FF), jnp.float32), jnp.zeros((FF, width), jnp.float32), jnp.zeros((width, 3 * width), jnp.float32), jnp.zeros((width, width), jnp.float32), jnp.zeros((width, 2 * width), jnp.float32), jnp.zeros((width, KW), jnp.float32), jnp.zeros((width,), jnp.float32), jnp.zeros((width,), jnp.float32), jnp.zeros((width,), jnp.float32), jnp.zeros((2, H), jnp.float32))
        lower_sums, dinput_seqs = lax.scan(lower_step, lower_init, (batch_tokens, batch_lengths, units_bn, dshifts, dconv_streams))
        outputs.append(out_lows)
        dinputs.append(dinput_seqs)
        gain_grads = jnp.stack([lower_sums[6], lower_sums[7], lower_sums[8], rear_sums[3], rear_sums[4], rear_sums[5]])
        step_grads = (lower_sums[0], lower_sums[1], lower_sums[2], lower_sums[3], lower_sums[4], lower_sums[5], rear_sums[2], rear_sums[0], rear_sums[1], gain_grads, rear_sums[6], lower_sums[9])
        totals = step_grads if totals is None else tuple((old + new for old, new in zip(totals, step_grads)))
    return (jnp.stack(outputs), jnp.stack(dinputs), totals[0], totals[1], totals[2], totals[3], totals[4], totals[5], totals[6], totals[7], totals[8], totals[9], totals[10], totals[11])
```

```python
import jax
import jax.numpy as jnp
from jax import lax
from jax.sharding import PartitionSpec as P

H = 8
HD = 64
RFAR = 256


EPS = 1e-05
NEGATIVE = -1e30


def extended(block, sides, width):
    for axis, dim in sides:
        count = lax.axis_size(axis)
        forward = [(i, i + 1) for i in range(count - 1)]
        backward = [(target, source) for source, target in forward]
        low = lax.ppermute(
            lax.slice_in_dim(block, block.shape[dim] - width, None, axis=dim), axis, forward
        )
        high = lax.ppermute(lax.slice_in_dim(block, 0, width, axis=dim), axis, backward)
        block = jnp.concatenate([low, block, high], axis=dim)
    return block


def product(left, right):
    return jnp.dot(left, right, preferred_element_type=jnp.float32)


def product_left(left, right):
    return jnp.dot(left.T, right, preferred_element_type=jnp.float32)


def product_right(left, right):
    return jnp.dot(left, right.T, preferred_element_type=jnp.float32)


def swish(value):
    return value * jax.nn.sigmoid(value)


def swish_slope(value):
    sigma = jax.nn.sigmoid(value)
    return sigma * (1.0 + value * (1.0 - sigma))


def layer_norm(stream, gain):
    centred = stream - jnp.mean(stream, axis=-1, keepdims=True)
    inverse = lax.rsqrt(jnp.mean(centred * centred, axis=-1, keepdims=True) + EPS)
    unit = centred * inverse
    return ((unit * gain).astype(jnp.bfloat16), unit, inverse)


def norm_back(dnormed, unit, inverse, gain):
    scaled = dnormed * gain
    dstream = inverse * (
        scaled
        - jnp.mean(scaled, axis=-1, keepdims=True)
        - unit * jnp.mean(scaled * unit, axis=-1, keepdims=True)
    )
    return (dstream, jnp.sum(dnormed * unit, axis=0))


def position_terms(query_start, rows, keys, head_terms):
    query_pos = query_start + lax.iota(jnp.int32, rows)
    key_pos = lax.iota(jnp.int32, keys)
    offset = query_pos[:, None] - key_pos[None, :]
    distance = jnp.abs(offset).astype(jnp.float32)
    far = (offset >= RFAR).astype(jnp.float32)
    bias = far[None] * head_terms[1][:, None, None] - distance[None] * head_terms[0][:, None, None]
    return (bias, distance, far)


def split_heads(queries, keyvals):
    rows, width = queries.shape
    keys = keyvals.shape[0]
    query_heads = queries.reshape(rows, H, HD)
    key_heads = keyvals[:, :width].reshape(keys, H, HD)
    value_heads = keyvals[:, width:].reshape(keys, H, HD)
    return (query_heads, key_heads, value_heads)


def score_heads(query_heads, key_heads, bias, key_valid):
    scores = jnp.einsum("qhd,khd->hqk", query_heads, key_heads, preferred_element_type=jnp.float32)
    scores = scores * HD ** (-0.5) + bias
    return jnp.where(key_valid[None, None, :], scores, NEGATIVE)


def attend_forward(queries, keyvals, bias, key_valid):
    rows, width = queries.shape
    query_heads, key_heads, value_heads = split_heads(queries, keyvals)
    scores = score_heads(query_heads, key_heads, bias, key_valid)
    top = jnp.max(scores, axis=-1, keepdims=True)
    logsum = top + jnp.log(jnp.sum(jnp.exp(scores - top), axis=-1, keepdims=True))
    probs = jnp.exp(scores - logsum).astype(jnp.bfloat16)
    context = jnp.einsum("hqk,khd->qhd", probs, value_heads, preferred_element_type=jnp.float32)
    return (context.reshape(rows, width).astype(jnp.bfloat16), logsum)


def attend_backward(queries, keyvals, bias, distance, far, key_valid, logsum, dcontext):
    rows, width = queries.shape
    keys = keyvals.shape[0]
    query_heads, key_heads, value_heads = split_heads(queries, keyvals)
    scores = score_heads(query_heads, key_heads, bias, key_valid)
    probs = jnp.exp(scores - logsum)
    dcontext_heads = dcontext.reshape(rows, H, HD)
    dprobs = jnp.einsum(
        "qhd,khd->hqk", dcontext_heads, value_heads, preferred_element_type=jnp.float32
    )
    dscores = probs * (dprobs - jnp.sum(probs * dprobs, axis=-1, keepdims=True))
    slope_grad = -jnp.sum(dscores * distance[None], axis=(1, 2))
    far_grad = jnp.sum(dscores * far[None], axis=(1, 2))
    dscores_low = dscores.astype(jnp.bfloat16)
    probs_low = probs.astype(jnp.bfloat16)
    factor = HD ** (-0.5)
    dquery = (
        jnp.einsum("hqk,khd->qhd", dscores_low, key_heads, preferred_element_type=jnp.float32)
        * factor
    )
    dkey = (
        jnp.einsum("hqk,qhd->khd", dscores_low, query_heads, preferred_element_type=jnp.float32)
        * factor
    )
    dvalue = jnp.einsum(
        "hqk,qhd->khd", probs_low, dcontext_heads, preferred_element_type=jnp.float32
    )
    dkeyvals = jnp.concatenate([dkey.reshape(keys, width), dvalue.reshape(keys, width)], axis=1)
    return (dquery.reshape(rows, width), dkeyvals, jnp.stack([slope_grad, far_grad]))


def depthwise_apply(padded, kernel, count):
    kernel_f = kernel.astype(jnp.float32)
    padded_f = padded.astype(jnp.float32)
    total = jnp.zeros(padded.shape[:-2] + (count, padded.shape[-1]), jnp.float32)
    for tap in range(kernel.shape[1]):
        total = total + padded_f[..., tap : tap + count, :] * kernel_f[:, tap]
    return total


def depthwise_back(padded, dpadded, ddepth, kernel, count):
    kernel_f = kernel.astype(jnp.float32)
    padded_f = padded.astype(jnp.float32)
    span = kernel.shape[1] - 1
    dgated = jnp.zeros(ddepth.shape, jnp.float32)
    columns = []
    for tap in range(kernel.shape[1]):
        dgated = dgated + dpadded[..., span - tap : span - tap + count, :] * kernel_f[:, tap]
        columns.append(
            jnp.sum(
                (padded_f[..., tap : tap + count, :] * ddepth).reshape(-1, kernel.shape[0]), axis=0
            )
        )
    return (dgated, jnp.stack(columns, axis=1))


def per_device(
    tokens,
    lengths,
    cotangent,
    first_up,
    first_down,
    project_in,
    project_out,
    pointwise_in,
    depthwise,
    pointwise_out,
    second_up,
    second_down,
    gains,
    batch_shift,
    head_terms,
):
    micro_count, seqs, local, width = tokens.shape
    rows = seqs * local
    full = local * lax.axis_size("ctx")
    half = depthwise.shape[1] // 2
    query_start = lax.axis_index("ctx") * local
    frame_pos = query_start + lax.iota(jnp.int32, local)
    key_pos = lax.iota(jnp.int32, full)
    bias, distance, far = position_terms(query_start, local, full, head_terms)
    outputs = []
    dinputs = []
    totals = None
    for micro in range(micro_count):
        front_weights = (
            lax.all_gather(first_up, "fsdp", axis=0, tiled=True),
            lax.all_gather(first_down, "fsdp", axis=0, tiled=True),
            lax.all_gather(project_in, "fsdp", axis=0, tiled=True),
            lax.all_gather(project_out, "fsdp", axis=0, tiled=True),
            lax.all_gather(pointwise_in, "fsdp", axis=0, tiled=True),
            lax.all_gather(depthwise, "fsdp", axis=0, tiled=True),
            lax.all_gather(pointwise_out, "fsdp", axis=0, tiled=True),
            lax.all_gather(second_up, "fsdp", axis=0, tiled=True),
            lax.all_gather(second_down, "fsdp", axis=0, tiled=True),
            lax.all_gather(gains, "fsdp", axis=1, tiled=True),
            lax.all_gather(batch_shift, "fsdp", axis=0, tiled=True),
        )
        (
            whole_first_up,
            whole_first_down,
            whole_project_in,
            whole_project_out,
            whole_pointwise_in,
            whole_depthwise,
            whole_pointwise_out,
            whole_second_up,
            whole_second_down,
            whole_gains,
            whole_shift,
        ) = front_weights
        gain_rows = whole_gains.astype(jnp.float32)
        shift_row = whole_shift.astype(jnp.float32)
        length_now = lengths[micro]
        mask = (frame_pos[None, :] < length_now[:, None]).astype(jnp.float32).reshape(rows, 1)
        key_valid = key_pos[None, :] < length_now[:, None]
        stream_in = tokens[micro].reshape(rows, width).astype(jnp.float32)
        normed_first, unit_first, inverse_first = layer_norm(stream_in, gain_rows[0])
        up_first = product(normed_first, whole_first_up)
        act_first = swish(up_first).astype(jnp.bfloat16)
        stream_first = stream_in + 0.5 * product(act_first, whole_first_down)
        normed_attend, unit_attend, inverse_attend = layer_norm(stream_first, gain_rows[1])
        triple = product(normed_attend, whole_project_in).astype(jnp.bfloat16)
        queries = triple[:, :width].reshape(seqs, local, width)
        keyvals = lax.all_gather(
            triple[:, width:].reshape(seqs, local, 2 * width), "ctx", axis=1, tiled=True
        )
        context, logsum = jax.vmap(attend_forward, in_axes=(0, 0, None, 0))(
            queries, keyvals, bias, key_valid
        )
        context = context.reshape(rows, width)
        stream_attend = stream_first + product(context, whole_project_out)
        normed_conv, unit_conv, inverse_conv = layer_norm(stream_attend, gain_rows[2])
        expanded = product(normed_conv, whole_pointwise_in)
        linear = expanded[:, :width]
        gate_sigma = jax.nn.sigmoid(expanded[:, width:])
        gated_low = (linear * gate_sigma * mask).astype(jnp.bfloat16).reshape(seqs, local, width)
        padded = extended(gated_low, (("ctx", 1),), half)
        depth = depthwise_apply(padded, whole_depthwise, local).reshape(rows, width)
        total, count = lax.psum((jnp.sum(mask * depth, axis=0), jnp.sum(mask)), ("fsdp", "ctx"))
        bn_mean = total / count
        centred_bn = depth - bn_mean
        spread = lax.psum(jnp.sum(mask * centred_bn * centred_bn, axis=0), ("fsdp", "ctx"))
        variance = spread / count
        inverse_bn = lax.rsqrt(variance + EPS)
        unit_bn = centred_bn * inverse_bn
        shifted = unit_bn * gain_rows[5] + shift_row
        act_conv = swish(shifted).astype(jnp.bfloat16)
        stream_conv = stream_attend + product(act_conv, whole_pointwise_out)
        normed_second, unit_second, inverse_second = layer_norm(stream_conv, gain_rows[3])
        up_second = product(normed_second, whole_second_up)
        act_second = swish(up_second).astype(jnp.bfloat16)
        stream_second = stream_conv + 0.5 * product(act_second, whole_second_down)
        out_low, unit_out, inverse_out = layer_norm(stream_second, gain_rows[4])
        outputs.append(out_low.reshape(seqs, local, width))
        back_weights = (
            lax.all_gather(first_up, "fsdp", axis=0, tiled=True),
            lax.all_gather(first_down, "fsdp", axis=0, tiled=True),
            lax.all_gather(project_in, "fsdp", axis=0, tiled=True),
            lax.all_gather(project_out, "fsdp", axis=0, tiled=True),
            lax.all_gather(pointwise_in, "fsdp", axis=0, tiled=True),
            lax.all_gather(depthwise, "fsdp", axis=0, tiled=True),
            lax.all_gather(pointwise_out, "fsdp", axis=0, tiled=True),
            lax.all_gather(second_up, "fsdp", axis=0, tiled=True),
            lax.all_gather(second_down, "fsdp", axis=0, tiled=True),
            lax.all_gather(gains, "fsdp", axis=1, tiled=True),
        )
        (
            back_first_up,
            back_first_down,
            back_project_in,
            back_project_out,
            back_pointwise_in,
            back_depthwise,
            back_pointwise_out,
            back_second_up,
            back_second_down,
            back_gains,
        ) = back_weights
        gain_rows = back_gains.astype(jnp.float32)
        dout = cotangent[micro].reshape(rows, width).astype(jnp.float32)
        dsecond_stream, gain_out = norm_back(dout, unit_out, inverse_out, gain_rows[4])
        dsecond_low = (0.5 * dsecond_stream).astype(jnp.bfloat16)
        dup_second = (product_right(dsecond_low, back_second_down) * swish_slope(up_second)).astype(
            jnp.bfloat16
        )
        dtemp, gain_second = norm_back(
            product_right(dup_second, back_second_up), unit_second, inverse_second, gain_rows[3]
        )
        dconv_stream = dsecond_stream + dtemp
        dconv_low = dconv_stream.astype(jnp.bfloat16)
        dshift = product_right(dconv_low, back_pointwise_out) * swish_slope(shifted)
        grad_shift = jnp.sum(dshift, axis=0)
        grad_gamma = jnp.sum(dshift * unit_bn, axis=0)
        sum_shift, sum_cross = lax.psum((grad_shift, grad_gamma), ("fsdp", "ctx"))
        ddepth = (
            inverse_bn
            * gain_rows[5]
            * (dshift - mask * sum_shift / count - mask * unit_bn * sum_cross / count)
        )
        ddepth = ddepth.reshape(seqs, local, width)
        dpadded = extended(ddepth.astype(jnp.bfloat16), (("ctx", 1),), half).astype(ddepth.dtype)
        dgated, grad_depth = depthwise_back(padded, dpadded, ddepth, back_depthwise, local)
        dgated = dgated.reshape(rows, width) * mask
        dexpanded = jnp.concatenate(
            [dgated * gate_sigma, dgated * linear * gate_sigma * (1.0 - gate_sigma)], axis=1
        ).astype(jnp.bfloat16)
        dtemp, gain_conv = norm_back(
            product_right(dexpanded, back_pointwise_in), unit_conv, inverse_conv, gain_rows[2]
        )
        dattend_stream = dconv_stream + dtemp
        dattend_low = dattend_stream.astype(jnp.bfloat16)
        dcontext = (
            product_right(dattend_low, back_project_out)
            .astype(jnp.bfloat16)
            .reshape(seqs, local, width)
        )
        dquery, dkeyvals_full, dheads = jax.vmap(
            attend_backward, in_axes=(0, 0, None, None, None, 0, 0, 0)
        )(queries, keyvals, bias, distance, far, key_valid, logsum, dcontext)
        dkeyvals = lax.psum_scatter(
            dkeyvals_full.astype(jnp.bfloat16), "ctx", scatter_dimension=1, tiled=True
        ).astype(jnp.float32)
        dtriple = (
            jnp.concatenate([dquery, dkeyvals], axis=2)
            .astype(jnp.bfloat16)
            .reshape(rows, 3 * width)
        )
        dtemp, gain_attend = norm_back(
            product_right(dtriple, back_project_in), unit_attend, inverse_attend, gain_rows[1]
        )
        dfirst_stream = dattend_stream + dtemp
        dfirst_low = (0.5 * dfirst_stream).astype(jnp.bfloat16)
        dup_first = (product_right(dfirst_low, back_first_down) * swish_slope(up_first)).astype(
            jnp.bfloat16
        )
        dtemp, gain_first = norm_back(
            product_right(dup_first, back_first_up), unit_first, inverse_first, gain_rows[0]
        )
        dinputs.append((dfirst_stream + dtemp).astype(jnp.bfloat16).reshape(seqs, local, width))
        gain_grads = jnp.stack(
            [gain_first, gain_attend, gain_conv, gain_second, gain_out, grad_gamma]
        )
        step_grads = (
            product_left(normed_first, dup_first),
            product_left(act_first, dfirst_low),
            product_left(normed_attend, dtriple),
            product_left(context, dattend_low),
            product_left(normed_conv, dexpanded),
            grad_depth,
            product_left(act_conv, dconv_low),
            product_left(normed_second, dup_second),
            product_left(act_second, dsecond_low),
            gain_grads,
            grad_shift,
            jnp.sum(dheads, axis=0),
        )
        totals = (
            step_grads
            if totals is None
            else tuple((old + new for old, new in zip(totals, step_grads)))
        )
    (
        grad_first_up,
        grad_first_down,
        grad_project_in,
        grad_project_out,
        grad_pointwise_in,
        grad_depthwise,
        grad_pointwise_out,
        grad_second_up,
        grad_second_down,
        grad_gains,
        grad_shift_all,
        grad_heads,
    ) = totals
    head_tile = jnp.broadcast_to(grad_heads[None], (lax.axis_size("fsdp"),) + grad_heads.shape)
    (
        shard_first_up,
        shard_first_down,
        shard_project_in,
        shard_project_out,
        shard_pointwise_in,
        shard_depthwise,
        shard_pointwise_out,
        shard_second_up,
        shard_second_down,
        shard_gains,
        shard_shift,
        shard_heads,
    ) = (
        lax.psum_scatter(grad_first_up.astype(jnp.bfloat16), "fsdp", scatter_dimension=0, tiled=True),
        lax.psum_scatter(grad_first_down.astype(jnp.bfloat16), "fsdp", scatter_dimension=0, tiled=True),
        lax.psum_scatter(grad_project_in.astype(jnp.bfloat16), "fsdp", scatter_dimension=0, tiled=True),
        lax.psum_scatter(grad_project_out.astype(jnp.bfloat16), "fsdp", scatter_dimension=0, tiled=True),
        lax.psum_scatter(grad_pointwise_in.astype(jnp.bfloat16), "fsdp", scatter_dimension=0, tiled=True),
        lax.psum_scatter(grad_depthwise, "fsdp", scatter_dimension=0, tiled=True),
        lax.psum_scatter(grad_pointwise_out.astype(jnp.bfloat16), "fsdp", scatter_dimension=0, tiled=True),
        lax.psum_scatter(grad_second_up.astype(jnp.bfloat16), "fsdp", scatter_dimension=0, tiled=True),
        lax.psum_scatter(grad_second_down.astype(jnp.bfloat16), "fsdp", scatter_dimension=0, tiled=True),
        lax.psum_scatter(grad_gains, "fsdp", scatter_dimension=1, tiled=True),
        lax.psum_scatter(grad_shift_all, "fsdp", scatter_dimension=0, tiled=True),
        lax.psum_scatter(head_tile, "fsdp", scatter_dimension=0, tiled=True),
    )
    summed = (
        lax.psum(shard_first_up.astype(jnp.bfloat16), "ctx").astype(jnp.float32),
        lax.psum(shard_first_down.astype(jnp.bfloat16), "ctx").astype(jnp.float32),
        lax.psum(shard_project_in.astype(jnp.bfloat16), "ctx").astype(jnp.float32),
        lax.psum(shard_project_out.astype(jnp.bfloat16), "ctx").astype(jnp.float32),
        lax.psum(shard_pointwise_in.astype(jnp.bfloat16), "ctx").astype(jnp.float32),
        lax.psum(shard_depthwise.astype(jnp.bfloat16), "ctx").astype(jnp.float32),
        lax.psum(shard_pointwise_out.astype(jnp.bfloat16), "ctx").astype(jnp.float32),
        lax.psum(shard_second_up.astype(jnp.bfloat16), "ctx").astype(jnp.float32),
        lax.psum(shard_second_down.astype(jnp.bfloat16), "ctx").astype(jnp.float32),
        lax.psum(shard_gains.astype(jnp.bfloat16), "ctx").astype(jnp.float32),
        lax.psum(shard_shift.astype(jnp.bfloat16), "ctx").astype(jnp.float32),
        lax.psum(shard_heads.astype(jnp.bfloat16), "ctx").astype(jnp.float32),
    )
    return (
        jnp.stack(outputs),
        jnp.stack(dinputs),
        summed[0],
        summed[1],
        summed[2],
        summed[3],
        summed[4],
        summed[5],
        summed[6],
        summed[7],
        summed[8],
        summed[9],
        summed[10],
        summed[11][0],
    )


def solution(mesh):
    in_specs = (
        P(None, "fsdp", "ctx", None),
        P(None, "fsdp"),
        P(None, "fsdp", "ctx", None),
        P("fsdp", None),
        P("fsdp", None),
        P("fsdp", None),
        P("fsdp", None),
        P("fsdp", None),
        P("fsdp", None),
        P("fsdp", None),
        P("fsdp", None),
        P("fsdp", None),
        P(None, "fsdp"),
        P("fsdp"),
        P(),
    )
    out_specs = (
        P(None, "fsdp", "ctx", None),
        P(None, "fsdp", "ctx", None),
        P("fsdp", None),
        P("fsdp", None),
        P("fsdp", None),
        P("fsdp", None),
        P("fsdp", None),
        P("fsdp", None),
        P("fsdp", None),
        P("fsdp", None),
        P("fsdp", None),
        P(None, "fsdp"),
        P("fsdp"),
        P(),
    )
    return jax.shard_map(
        per_device, mesh=mesh, in_specs=in_specs, out_specs=out_specs, check_vma=False
    )
```

```python
import jax
import jax.numpy as jnp
from jax import lax
from jax.sharding import PartitionSpec as P

H = 8
HD = 64
RFAR = 256


EPS = 1e-05
NEGATIVE = -1e30


def extended(block, sides, width):
    for axis, dim in sides:
        count = lax.axis_size(axis)
        forward = [(i, i + 1) for i in range(count - 1)]
        backward = [(target, source) for source, target in forward]
        low = lax.ppermute(
            lax.slice_in_dim(block, block.shape[dim] - width, None, axis=dim), axis, forward
        )
        high = lax.ppermute(lax.slice_in_dim(block, 0, width, axis=dim), axis, backward)
        block = jnp.concatenate([low, block, high], axis=dim)
    return block


def product(left, right):
    return jnp.dot(left, right, preferred_element_type=jnp.float32)


def product_left(left, right):
    return jnp.dot(left.T, right, preferred_element_type=jnp.float32)


def product_right(left, right):
    return jnp.dot(left, right.T, preferred_element_type=jnp.float32)


def swish(value):
    return value * jax.nn.sigmoid(value)


def swish_slope(value):
    sigma = jax.nn.sigmoid(value)
    return sigma * (1.0 + value * (1.0 - sigma))


def layer_norm(stream, gain):
    centred = stream - jnp.mean(stream, axis=-1, keepdims=True)
    inverse = lax.rsqrt(jnp.mean(centred * centred, axis=-1, keepdims=True) + EPS)
    unit = centred * inverse
    return ((unit * gain).astype(jnp.bfloat16), unit, inverse)


def norm_back(dnormed, unit, inverse, gain):
    scaled = dnormed * gain
    dstream = inverse * (
        scaled
        - jnp.mean(scaled, axis=-1, keepdims=True)
        - unit * jnp.mean(scaled * unit, axis=-1, keepdims=True)
    )
    return (dstream, jnp.sum(dnormed * unit, axis=0))


def position_terms(query_start, rows, keys, head_terms):
    query_pos = query_start + lax.iota(jnp.int32, rows)
    key_pos = lax.iota(jnp.int32, keys)
    offset = query_pos[:, None] - key_pos[None, :]
    distance = jnp.abs(offset).astype(jnp.float32)
    far = (offset >= RFAR).astype(jnp.float32)
    bias = far[None] * head_terms[1][:, None, None] - distance[None] * head_terms[0][:, None, None]
    return (bias, distance, far)


def split_heads(queries, keyvals):
    rows, width = queries.shape
    keys = keyvals.shape[0]
    query_heads = queries.reshape(rows, H, HD)
    key_heads = keyvals[:, :width].reshape(keys, H, HD)
    value_heads = keyvals[:, width:].reshape(keys, H, HD)
    return (query_heads, key_heads, value_heads)


def score_heads(query_heads, key_heads, bias, key_valid):
    scores = jnp.einsum("qhd,khd->hqk", query_heads, key_heads, preferred_element_type=jnp.float32)
    scores = scores * HD ** (-0.5) + bias
    return jnp.where(key_valid[None, None, :], scores, NEGATIVE)


def attend_forward(queries, keyvals, bias, key_valid):
    rows, width = queries.shape
    query_heads, key_heads, value_heads = split_heads(queries, keyvals)
    scores = score_heads(query_heads, key_heads, bias, key_valid)
    top = jnp.max(scores, axis=-1, keepdims=True)
    logsum = top + jnp.log(jnp.sum(jnp.exp(scores - top), axis=-1, keepdims=True))
    probs = jnp.exp(scores - logsum).astype(jnp.bfloat16)
    context = jnp.einsum("hqk,khd->qhd", probs, value_heads, preferred_element_type=jnp.float32)
    return (context.reshape(rows, width).astype(jnp.bfloat16), logsum)


def attend_backward(queries, keyvals, bias, distance, far, key_valid, logsum, dcontext):
    rows, width = queries.shape
    keys = keyvals.shape[0]
    query_heads, key_heads, value_heads = split_heads(queries, keyvals)
    scores = score_heads(query_heads, key_heads, bias, key_valid)
    probs = jnp.exp(scores - logsum)
    dcontext_heads = dcontext.reshape(rows, H, HD)
    dprobs = jnp.einsum(
        "qhd,khd->hqk", dcontext_heads, value_heads, preferred_element_type=jnp.float32
    )
    dscores = probs * (dprobs - jnp.sum(probs * dprobs, axis=-1, keepdims=True))
    slope_grad = -jnp.sum(dscores * distance[None], axis=(1, 2))
    far_grad = jnp.sum(dscores * far[None], axis=(1, 2))
    dscores_low = dscores.astype(jnp.bfloat16)
    probs_low = probs.astype(jnp.bfloat16)
    factor = HD ** (-0.5)
    dquery = (
        jnp.einsum("hqk,khd->qhd", dscores_low, key_heads, preferred_element_type=jnp.float32)
        * factor
    )
    dkey = (
        jnp.einsum("hqk,qhd->khd", dscores_low, query_heads, preferred_element_type=jnp.float32)
        * factor
    )
    dvalue = jnp.einsum(
        "hqk,qhd->khd", probs_low, dcontext_heads, preferred_element_type=jnp.float32
    )
    dkeyvals = jnp.concatenate([dkey.reshape(keys, width), dvalue.reshape(keys, width)], axis=1)
    return (dquery.reshape(rows, width), dkeyvals, jnp.stack([slope_grad, far_grad]))


def depthwise_apply(padded, kernel, count):
    kernel_f = kernel.astype(jnp.float32)
    padded_f = padded.astype(jnp.float32)
    total = jnp.zeros(padded.shape[:-2] + (count, padded.shape[-1]), jnp.float32)
    for tap in range(kernel.shape[1]):
        total = total + padded_f[..., tap : tap + count, :] * kernel_f[:, tap]
    return total


def depthwise_back(padded, dpadded, ddepth, kernel, count):
    kernel_f = kernel.astype(jnp.float32)
    padded_f = padded.astype(jnp.float32)
    span = kernel.shape[1] - 1
    dgated = jnp.zeros(ddepth.shape, jnp.float32)
    columns = []
    for tap in range(kernel.shape[1]):
        dgated = dgated + dpadded[..., span - tap : span - tap + count, :] * kernel_f[:, tap]
        columns.append(
            jnp.sum(
                (padded_f[..., tap : tap + count, :] * ddepth).reshape(-1, kernel.shape[0]), axis=0
            )
        )
    return (dgated, jnp.stack(columns, axis=1))


def column_blocks(stack, width):
    extra = -stack.shape[2] % width
    if extra:
        stack = jnp.pad(stack, ((0, 0), (0, 0), (0, extra)))
    return [stack[:, :, at : at + width] for at in range(0, stack.shape[2], width)]


def per_device(
    tokens,
    lengths,
    cotangent,
    first_up,
    first_down,
    project_in,
    project_out,
    pointwise_in,
    depthwise,
    pointwise_out,
    second_up,
    second_down,
    gains,
    batch_shift,
    head_terms,
):
    micro_count, seqs, local, width = tokens.shape
    rows = seqs * local
    full = local * lax.axis_size("ctx")
    half = depthwise.shape[1] // 2
    query_start = lax.axis_index("ctx") * local
    frame_pos = query_start + lax.iota(jnp.int32, local)
    key_pos = lax.iota(jnp.int32, full)
    bias, distance, far = position_terms(query_start, local, full, head_terms)
    taps = depthwise.shape[1]
    gain_count = gains.shape[0]
    small_params = lax.all_gather(
        jnp.concatenate([depthwise, gains.T, batch_shift[:, None]], axis=1),
        "fsdp",
        axis=0,
        tiled=True,
    )
    all_depthwise = small_params[:, :taps]
    all_gains = small_params[:, taps : taps + gain_count].T
    all_shift = small_params[:, taps + gain_count]
    outputs = []
    dinputs = []
    totals = None
    for micro in range(micro_count):
        front_weights = (
            lax.all_gather(first_up, "fsdp", axis=0, tiled=True),
            lax.all_gather(first_down, "fsdp", axis=0, tiled=True),
            lax.all_gather(project_in, "fsdp", axis=0, tiled=True),
            lax.all_gather(project_out, "fsdp", axis=0, tiled=True),
            lax.all_gather(pointwise_in, "fsdp", axis=0, tiled=True),
            all_depthwise,
            lax.all_gather(pointwise_out, "fsdp", axis=0, tiled=True),
            lax.all_gather(second_up, "fsdp", axis=0, tiled=True),
            lax.all_gather(second_down, "fsdp", axis=0, tiled=True),
            all_gains,
            all_shift,
        )
        (
            whole_first_up,
            whole_first_down,
            whole_project_in,
            whole_project_out,
            whole_pointwise_in,
            whole_depthwise,
            whole_pointwise_out,
            whole_second_up,
            whole_second_down,
            whole_gains,
            whole_shift,
        ) = front_weights
        gain_rows = whole_gains.astype(jnp.float32)
        shift_row = whole_shift.astype(jnp.float32)
        length_now = lengths[micro]
        mask = (frame_pos[None, :] < length_now[:, None]).astype(jnp.float32).reshape(rows, 1)
        key_valid = key_pos[None, :] < length_now[:, None]
        stream_in = tokens[micro].reshape(rows, width).astype(jnp.float32)
        normed_first, unit_first, inverse_first = layer_norm(stream_in, gain_rows[0])
        up_first = product(normed_first, whole_first_up)
        act_first = swish(up_first).astype(jnp.bfloat16)
        stream_first = stream_in + 0.5 * product(act_first, whole_first_down)
        normed_attend, unit_attend, inverse_attend = layer_norm(stream_first, gain_rows[1])
        triple = product(normed_attend, whole_project_in).astype(jnp.bfloat16)
        queries = triple[:, :width].reshape(seqs, local, width)
        keyvals = lax.all_gather(
            triple[:, width:].reshape(seqs, local, 2 * width), "ctx", axis=1, tiled=True
        )
        context, logsum = jax.vmap(attend_forward, in_axes=(0, 0, None, 0))(
            queries, keyvals, bias, key_valid
        )
        context = context.reshape(rows, width)
        stream_attend = stream_first + product(context, whole_project_out)
        normed_conv, unit_conv, inverse_conv = layer_norm(stream_attend, gain_rows[2])
        expanded = product(normed_conv, whole_pointwise_in)
        linear = expanded[:, :width]
        gate_sigma = jax.nn.sigmoid(expanded[:, width:])
        gated_low = (linear * gate_sigma * mask).astype(jnp.bfloat16).reshape(seqs, local, width)
        padded = extended(gated_low, (("ctx", 1),), half)
        depth = depthwise_apply(padded, whole_depthwise, local).reshape(rows, width)
        total, count = lax.psum((jnp.sum(mask * depth, axis=0), jnp.sum(mask)), ("fsdp", "ctx"))
        bn_mean = total / count
        centred_bn = depth - bn_mean
        spread = lax.psum(jnp.sum(mask * centred_bn * centred_bn, axis=0), ("fsdp", "ctx"))
        variance = spread / count
        inverse_bn = lax.rsqrt(variance + EPS)
        unit_bn = centred_bn * inverse_bn
        shifted = unit_bn * gain_rows[5] + shift_row
        act_conv = swish(shifted).astype(jnp.bfloat16)
        stream_conv = stream_attend + product(act_conv, whole_pointwise_out)
        normed_second, unit_second, inverse_second = layer_norm(stream_conv, gain_rows[3])
        up_second = product(normed_second, whole_second_up)
        act_second = swish(up_second).astype(jnp.bfloat16)
        stream_second = stream_conv + 0.5 * product(act_second, whole_second_down)
        out_low, unit_out, inverse_out = layer_norm(stream_second, gain_rows[4])
        outputs.append(out_low.reshape(seqs, local, width))
        back_weights = (
            lax.all_gather(first_up, "fsdp", axis=0, tiled=True),
            lax.all_gather(first_down, "fsdp", axis=0, tiled=True),
            lax.all_gather(project_in, "fsdp", axis=0, tiled=True),
            lax.all_gather(project_out, "fsdp", axis=0, tiled=True),
            lax.all_gather(pointwise_in, "fsdp", axis=0, tiled=True),
            all_depthwise,
            lax.all_gather(pointwise_out, "fsdp", axis=0, tiled=True),
            lax.all_gather(second_up, "fsdp", axis=0, tiled=True),
            lax.all_gather(second_down, "fsdp", axis=0, tiled=True),
            all_gains,
        )
        (
            back_first_up,
            back_first_down,
            back_project_in,
            back_project_out,
            back_pointwise_in,
            back_depthwise,
            back_pointwise_out,
            back_second_up,
            back_second_down,
            back_gains,
        ) = back_weights
        gain_rows = back_gains.astype(jnp.float32)
        dout = cotangent[micro].reshape(rows, width).astype(jnp.float32)
        dsecond_stream, gain_out = norm_back(dout, unit_out, inverse_out, gain_rows[4])
        dsecond_low = (0.5 * dsecond_stream).astype(jnp.bfloat16)
        dup_second = (product_right(dsecond_low, back_second_down) * swish_slope(up_second)).astype(
            jnp.bfloat16
        )
        dtemp, gain_second = norm_back(
            product_right(dup_second, back_second_up), unit_second, inverse_second, gain_rows[3]
        )
        dconv_stream = dsecond_stream + dtemp
        dconv_low = dconv_stream.astype(jnp.bfloat16)
        dshift = product_right(dconv_low, back_pointwise_out) * swish_slope(shifted)
        grad_shift = jnp.sum(dshift, axis=0)
        grad_gamma = jnp.sum(dshift * unit_bn, axis=0)
        sum_shift, sum_cross = lax.psum((grad_shift, grad_gamma), ("fsdp", "ctx"))
        ddepth = (
            inverse_bn
            * gain_rows[5]
            * (dshift - mask * sum_shift / count - mask * unit_bn * sum_cross / count)
        )
        ddepth = ddepth.reshape(seqs, local, width)
        dpadded = extended(ddepth.astype(jnp.bfloat16), (("ctx", 1),), half).astype(ddepth.dtype)
        dgated, grad_depth = depthwise_back(padded, dpadded, ddepth, back_depthwise, local)
        dgated = dgated.reshape(rows, width) * mask
        dexpanded = jnp.concatenate(
            [dgated * gate_sigma, dgated * linear * gate_sigma * (1.0 - gate_sigma)], axis=1
        ).astype(jnp.bfloat16)
        dtemp, gain_conv = norm_back(
            product_right(dexpanded, back_pointwise_in), unit_conv, inverse_conv, gain_rows[2]
        )
        dattend_stream = dconv_stream + dtemp
        dattend_low = dattend_stream.astype(jnp.bfloat16)
        dcontext = (
            product_right(dattend_low, back_project_out)
            .astype(jnp.bfloat16)
            .reshape(seqs, local, width)
        )
        dquery, dkeyvals_full, dheads = jax.vmap(
            attend_backward, in_axes=(0, 0, None, None, None, 0, 0, 0)
        )(queries, keyvals, bias, distance, far, key_valid, logsum, dcontext)
        dkeyvals = lax.psum_scatter(
            dkeyvals_full.astype(jnp.bfloat16), "ctx", scatter_dimension=1, tiled=True
        ).astype(jnp.float32)
        dtriple = (
            jnp.concatenate([dquery, dkeyvals], axis=2)
            .astype(jnp.bfloat16)
            .reshape(rows, 3 * width)
        )
        dtemp, gain_attend = norm_back(
            product_right(dtriple, back_project_in), unit_attend, inverse_attend, gain_rows[1]
        )
        dfirst_stream = dattend_stream + dtemp
        dfirst_low = (0.5 * dfirst_stream).astype(jnp.bfloat16)
        dup_first = (product_right(dfirst_low, back_first_down) * swish_slope(up_first)).astype(
            jnp.bfloat16
        )
        dtemp, gain_first = norm_back(
            product_right(dup_first, back_first_up), unit_first, inverse_first, gain_rows[0]
        )
        dinputs.append((dfirst_stream + dtemp).astype(jnp.bfloat16).reshape(seqs, local, width))
        gain_grads = jnp.stack(
            [gain_first, gain_attend, gain_conv, gain_second, gain_out, grad_gamma]
        )
        step_grads = (
            product_left(normed_first, dup_first),
            product_left(act_first, dfirst_low),
            product_left(normed_attend, dtriple),
            product_left(context, dattend_low),
            product_left(normed_conv, dexpanded),
            grad_depth,
            product_left(act_conv, dconv_low),
            product_left(normed_second, dup_second),
            product_left(act_second, dsecond_low),
            gain_grads,
            grad_shift,
            jnp.sum(dheads, axis=0),
        )
        totals = (
            step_grads
            if totals is None
            else tuple((old + new for old, new in zip(totals, step_grads)))
        )
    (
        grad_first_up,
        grad_first_down,
        grad_project_in,
        grad_project_out,
        grad_pointwise_in,
        grad_depthwise,
        grad_pointwise_out,
        grad_second_up,
        grad_second_down,
        grad_gains,
        grad_shift_all,
        grad_heads,
    ) = totals
    shards = lax.axis_size("fsdp")
    gain_count = grad_gains.shape[0]
    small = jnp.concatenate(
        [grad_depthwise, grad_gains.T, grad_shift_all[:, None]], axis=1
    )
    heads_flat = jnp.broadcast_to(grad_heads.reshape(1, 1, -1), (shards, 1, grad_heads.size))
    weight_grads = (
        grad_first_up,
        grad_first_down,
        grad_project_in,
        grad_project_out,
        grad_pointwise_in,
        grad_pointwise_out,
        grad_second_up,
        grad_second_down,
        small,
    )
    pieces = []
    for grad in weight_grads:
        pieces.extend(column_blocks(grad.astype(jnp.bfloat16).reshape(shards, -1, grad.shape[1]), width))
    pieces.extend(column_blocks(heads_flat.astype(jnp.bfloat16), width))
    packed = jnp.concatenate(pieces, axis=1)
    shard = lax.psum_scatter(packed, "fsdp", scatter_dimension=0, tiled=True)
    summed_pack = lax.psum(shard[0], "ctx").astype(jnp.float32)
    start = 0
    unpacked = []
    for grad in weight_grads:
        rows_here = grad.shape[0] // shards
        blocks = []
        for column in range(0, grad.shape[1], width):
            blocks.append(summed_pack[start : start + rows_here])
            start += rows_here
        unpacked.append(jnp.concatenate(blocks, axis=1)[:, : grad.shape[1]])
    heads_row = summed_pack[start, : grad_heads.size].reshape(grad_heads.shape)
    taps = depthwise.shape[1]
    small_sum = unpacked[8]
    summed = (
        unpacked[0],
        unpacked[1],
        unpacked[2],
        unpacked[3],
        unpacked[4],
        small_sum[:, :taps],
        unpacked[5],
        unpacked[6],
        unpacked[7],
        small_sum[:, taps : taps + gain_count].T,
        small_sum[:, taps + gain_count],
        heads_row[None],
    )
    return (
        jnp.stack(outputs),
        jnp.stack(dinputs),
        summed[0],
        summed[1],
        summed[2],
        summed[3],
        summed[4],
        summed[5],
        summed[6],
        summed[7],
        summed[8],
        summed[9],
        summed[10],
        summed[11][0],
    )


def solution(mesh):
    in_specs = (
        P(None, "fsdp", "ctx", None),
        P(None, "fsdp"),
        P(None, "fsdp", "ctx", None),
        P("fsdp", None),
        P("fsdp", None),
        P("fsdp", None),
        P("fsdp", None),
        P("fsdp", None),
        P("fsdp", None),
        P("fsdp", None),
        P("fsdp", None),
        P("fsdp", None),
        P(None, "fsdp"),
        P("fsdp"),
        P(),
    )
    out_specs = (
        P(None, "fsdp", "ctx", None),
        P(None, "fsdp", "ctx", None),
        P("fsdp", None),
        P("fsdp", None),
        P("fsdp", None),
        P("fsdp", None),
        P("fsdp", None),
        P("fsdp", None),
        P("fsdp", None),
        P("fsdp", None),
        P("fsdp", None),
        P(None, "fsdp"),
        P("fsdp"),
        P(),
    )
    return jax.shard_map(
        per_device, mesh=mesh, in_specs=in_specs, out_specs=out_specs, check_vma=False
    )
```
